512 devices in a mesh: row: 8 (over z_lo), col: 16 (over x, y), layer: 4 (over z_hi, core).
Axes of the slice: x: 4, y: 4, z: 16 (z_hi: 2, z_lo: 8; z = z_hi * 8 + z_lo), core: 2. Of those that a mesh axis runs over, the one named last changes fastest.
Arguments:
- doubles_amplitude_tensor: float32 [2304, 2048], P('col', 'layer'), may hold values from -6 to 6
- integrals: float32 [8, 16, 4, 96, 2048], P('row', 'col', 'layer'), may hold values from -0.125 to 0.125
- incoming_residual: float32 [2304, 49152], P('col', ('row', 'layer')), may hold values from -6 to 6
Outputs:
- updated_residual: float32 [2304, 49152], P('col', ('row', 'layer'))
The draws below stay inside these ranges and needn't reach their ends.
All inputs are finite; a program needn't handle non-finite values.
Results may differ from the reference program's by a relative error of at most 0.00005.
Values sent between devices are 32-bit elements; how exact they have to be, the bound alone decides.
No kernel may reach another device: no remote copies, remote signals or barrier semaphores. Data moves between devices by JAX's collectives and lax.ppermute only.
A program may use at most 64 MiB of HBM per device.

```python
import jax
import jax.numpy as jnp
from jax import lax

AB_DEV = 96
IJ = 2304
CD = 2048
AB = 49152
N_ROW = 8
N_COL = 16
N_LAYER = 4


def block_scale(rng, dims, split, least, top_value):
    def one(dim, shards_of):
        draws = jax.random.uniform(jax.random.fold_in(jax.random.fold_in(rng, 6), dim), (shards_of,), jnp.float32, least / len(split), top_value / len(split))
        return jnp.repeat(jnp.exp(draws), dims[dim] // shards_of).reshape((-1,) + (1,) * (len(dims) - dim - 1))

    factor_of = one(*split[0])
    for cut in split[1:]:
        factor_of = factor_of * one(*cut)
    return factor_of


def normal_values(key, extent, deviation, bound, split=(), dtype=jnp.bfloat16):
    entries = jax.random.normal(key, extent, jnp.float32) * deviation
    if len(split) > 0:
        entries = block_scale(key, extent, split, -0.22, 0.18) * entries
    return jnp.clip(entries, min=-bound, max=bound).astype(dtype)


def setup_inputs(seed: int = 0) -> dict:
    streams_of = jax.random.split(jax.random.key(seed), 4)
    doubles_amplitude_tensor = normal_values(streams_of[0], (IJ, CD), 1.0, 6.0, ((0, 16), (1, 4)), jnp.float32)
    integrals = normal_values(streams_of[1], (N_ROW, N_COL, N_LAYER, AB_DEV, CD), CD ** -0.5, 0.125, ((0, 8), (1, 16), (2, 4)), jnp.float32)
    incoming_residual = normal_values(streams_of[2], (IJ, AB), 1.0, 6.0, ((0, 16), (1, 32)), jnp.float32)
    return {"doubles_amplitude_tensor": doubles_amplitude_tensor, "integrals": integrals, "incoming_residual": incoming_residual}


def reference(doubles_amplitude_tensor, integrals, incoming_residual):
    sorted_pieces = jnp.transpose(integrals, (0, 2, 1, 3, 4))
    virtual_integral_matrix = sorted_pieces.reshape(-1, integrals.shape[4])
    ladder_contribution = lax.dot_general(doubles_amplitude_tensor, virtual_integral_matrix, (((1,), (1,)), ((), ())), precision=lax.Precision.HIGHEST, preferred_element_type=jnp.float32)
    return incoming_residual + ladder_contribution
```

```python
import functools

import jax
import jax.numpy as jnp
from jax import lax
from jax.experimental import pallas as pl
from jax.experimental.pallas import tpu as pltpu
from jax.sharding import PartitionSpec as P

AXES = ("row", "col", "layer")
SIDE = 4
LIMIT = 24 * 2**20
FAKE = 30 * 10**9
PRICE = 20.0
GATE = 20 * 10**9


def device_of(x, y, z, core):
    return ((z % 8) * 16 + (x % 4) * 4 + y % 4) * 4 + (z % 16 // 8) * 2 + core


def shifted(dx=0, dz=0, swap=False):
    return [
        (device_of(x, y, z, core), device_of(x + dx, y, z + dz, 1 - core if swap else core))
        for x in range(4)
        for y in range(4)
        for z in range(16)
        for core in range(2)
    ]


Y_RINGS = [[x * SIDE + y for y in range(SIDE)] for x in range(SIDE)]
Y_RINGS_OF_TWO = [
    [(row + part) * 16 + x * SIDE + y for part in range(2) for y in range(SIDE)]
    for row in range(0, 8, 2)
    for x in range(SIDE)
]


def halves(value):
    high = value.astype(jnp.bfloat16)
    return high, (value - high.astype(jnp.float32)).astype(jnp.bfloat16)


def times(a, b):
    def one(p, q):
        return lax.dot_general(p, q, (((1,), (1,)), ((), ())), preferred_element_type=jnp.float32)

    (a_high, a_low), (b_high, b_low) = halves(a), halves(b)
    return one(a_high, b_high) + (one(a_high, b_low) + one(a_low, b_high))


def ladder_kernel(turns, accumulate, *refs):
    if accumulate:
        so_far, refs = refs[0], refs[1:]
    terms, blocks, out = refs[: len(turns)], refs[len(turns) : len(turns) + SIDE], refs[-1]
    layer = lax.axis_index("layer")
    ys, rows, _ = out.shape
    total = None
    for (far, swapped), t_ref in zip(turns, terms, strict=True):
        at_layer = ((layer // 2) ^ far) * 2 + ((layer % 2) ^ swapped)
        pieces, _, width = t_ref.shape
        at = pl.ds(pl.multiple_of(at_layer * width, width), width)
        v = jnp.concatenate([b[:, at] for b in blocks], axis=0)
        t = jnp.concatenate([t_ref[part * ys + y] for y in range(ys) for part in range(pieces // ys)], axis=0)
        total = times(t, v) if total is None else total + times(t, v)
    total = total.reshape(out.shape)
    out[...] = so_far[...] + total if accumulate else total


def ladder(turns, so_far, terms, blocks, shape, name, price=1.0, after=()):
    columns = sum(b.shape[0] for b in blocks)
    given = (() if so_far is None else (so_far,)) + (*terms, *blocks)
    flops = 2 * 3 * shape[0] * shape[1] * columns * len(turns) * terms[0].shape[-1]
    return pl.pallas_call(
        functools.partial(ladder_kernel, turns, so_far is not None),
        out_shape=jax.ShapeDtypeStruct(shape, jnp.float32),
        in_specs=[pl.BlockSpec(memory_space=pltpu.VMEM)] * len(given)
        + [pl.BlockSpec(memory_space=pl.ANY)] * len(after),
        out_specs=pl.BlockSpec(memory_space=pltpu.VMEM),
        cost_estimate=pl.CostEstimate(
            flops=int(flops * price),
            bytes_accessed=4 * sum(a.size for a in given) + 4 * shape[0] * shape[1] * shape[2],
            transcendentals=0,
        ),
        compiler_params=pltpu.CompilerParams(vmem_limit_bytes=LIMIT),
        name=name,
    )(*given, *after)


def gate_kernel(*refs):
    refs[-1][...] = jnp.zeros_like(refs[-1])


def gate(values, price):
    return pl.pallas_call(
        gate_kernel,
        out_shape=jax.ShapeDtypeStruct((8, 128), jnp.float32),
        in_specs=[pl.BlockSpec(memory_space=pl.ANY)] * len(values),
        out_specs=pl.BlockSpec(memory_space=pltpu.VMEM),
        cost_estimate=pl.CostEstimate(flops=price, bytes_accessed=4096, transcendentals=0),
        compiler_params=pltpu.CompilerParams(vmem_limit_bytes=LIMIT),
        name="arrived",
    )(*values)


def spread_kernel(given, out):
    for place in range(out.shape[0]):
        out[place] = given[...]


def spread(value, copies, name, price=0):
    return pl.pallas_call(
        spread_kernel,
        out_shape=jax.ShapeDtypeStruct((copies, *value.shape), jnp.float32),
        in_specs=[pl.BlockSpec(memory_space=pltpu.VMEM)],
        out_specs=pl.BlockSpec(memory_space=pltpu.VMEM),
        cost_estimate=pl.CostEstimate(
            flops=price, bytes_accessed=4 * value.size * (1 + copies), transcendentals=0
        ),
        compiler_params=pltpu.CompilerParams(vmem_limit_bytes=LIMIT),
        name=name,
    )(value)


def add_kernel(order, residual, parts, out):
    x = lax.axis_index("col") // SIDE
    ys, _, columns = parts.shape
    each = columns // SIDE
    for place, step in enumerate(order):
        at = pl.ds(pl.multiple_of((x + step) % SIDE * columns, columns), columns)
        block = jnp.concatenate([parts[y, :, place * each : (place + 1) * each] for y in range(ys)], axis=1)
        out[:, at] = residual[:, at] + block


def add(order, residual, parts):
    import functools

    return pl.pallas_call(
        functools.partial(add_kernel, order),
        out_shape=jax.ShapeDtypeStruct(residual.shape, jnp.float32),
        in_specs=[pl.BlockSpec(memory_space=pltpu.VMEM)] * 2,
        out_specs=pl.BlockSpec(memory_space=pltpu.VMEM),
        compiler_params=pltpu.CompilerParams(vmem_limit_bytes=LIMIT),
        name="add_ladder",
    )(residual, parts)


def on_device(t, integrals, residual):
    v = integrals.reshape(integrals.shape[3:])
    rows, width = t.shape

    def send(value, **move):
        return lax.ppermute(value, AXES, shifted(**move))

    def along_y(value):
        whole = spread(value, SIDE, "spread_near")
        return lax.all_to_all(whole, "col", 0, 0, axis_index_groups=Y_RINGS)

    def along_two(whole):
        return lax.all_to_all(whole, ("row", "col"), 0, 0, axis_index_groups=Y_RINGS_OF_TWO)

    share = lax.dynamic_slice_in_dim(t, lax.axis_index("row") % 2 * (rows // 2), rows // 2, 0)
    share_far = send(share, dz=8)
    v_left, v_right = send(v, dx=1), send(v, dx=-1)
    near = along_y(t)
    share_far = spread(share_far, 2 * SIDE, "spread_far", FAKE)
    share_far, v_left, v_right, v_next = lax.optimization_barrier((share_far, v_left, v_right, v))
    v_across = send(v_next, dx=2)
    near_pair = send(near, swap=True)
    far = along_two(share_far)
    order = (0, -1, 1, 2)
    blocks = (v, v_left, v_right, v_across)
    shape = (SIDE, rows, SIDE * v.shape[0])
    total = ladder(((0, 0), (0, 1)), None, (near, near_pair), blocks, shape, "ladder_near", PRICE, (gate((v_across,), GATE),))
    far, total = lax.optimization_barrier((far, total))
    far_pair = send(far, swap=True)
    total = ladder(((1, 0),), total, (far,), blocks, shape, "ladder_far")
    total = ladder(((1, 1),), total, (far_pair,), blocks, shape, "ladder_far_pair")
    parts = lax.all_to_all(total, "col", 0, 0, axis_index_groups=Y_RINGS)
    return add(order, residual, parts)


def solution(mesh):
    return jax.shard_map(
        on_device,
        mesh=mesh,
        in_specs=(
            P("col", "layer"),
            P("row", "col", "layer", None, None),
            P("col", ("row", "layer")),
        ),
        out_specs=P("col", ("row", "layer")),
        check_vma=False,
    )
```

```python
import functools

import jax
import jax.numpy as jnp
from jax import lax
from jax.experimental import pallas as pl
from jax.experimental.pallas import tpu as pltpu
from jax.sharding import PartitionSpec as P

AXES = ("row", "col", "layer")
SIDE = 4
LIMIT = 24 * 2**20
FAKE = 12 * 10**9
PRICE = 20.0
GATE = 10 * 10**9


def device_of(x, y, z, core):
    return ((z % 8) * 16 + (x % 4) * 4 + y % 4) * 4 + (z % 16 // 8) * 2 + core


def shifted(dx=0, mirror=False, swap=False):
    return [
        (
            device_of(x, y, z, core),
            device_of(x + dx, y, 15 - z if mirror else z, 1 - core if swap else core),
        )
        for x in range(4)
        for y in range(4)
        for z in range(16)
        for core in range(2)
    ]


Y_RINGS = [[x * SIDE + y for y in range(SIDE)] for x in range(SIDE)]
Y_RINGS_OF_TWO = [
    [(row + part) * 16 + x * SIDE + y for part in range(2) for y in range(SIDE)]
    for row in range(0, 8, 2)
    for x in range(SIDE)
]


def halves(value):
    high = value.astype(jnp.bfloat16)
    return high, (value - high.astype(jnp.float32)).astype(jnp.bfloat16)


def times(a, b):
    def one(p, q):
        return lax.dot_general(p, q, (((1,), (1,)), ((), ())), preferred_element_type=jnp.float32)

    (a_high, a_low), (b_high, b_low) = halves(a), halves(b)
    return one(a_high, b_high) + (one(a_high, b_low) + one(a_low, b_high))


def ladder_kernel(turns, accumulate, n_blocks, *refs):
    if accumulate:
        so_far, refs = refs[0], refs[1:]
    terms, blocks, out = refs[: len(turns)], refs[len(turns) : len(turns) + n_blocks], refs[-1]
    layer = lax.axis_index("layer")
    ys, rows, _ = out.shape
    total = None
    for (far, swapped), t_ref in zip(turns, terms, strict=True):
        at_layer = ((layer // 2) ^ far) * 2 + ((layer % 2) ^ swapped)
        pieces, _, width = t_ref.shape
        at = pl.ds(pl.multiple_of(at_layer * width, width), width)
        v = jnp.concatenate([b[:, at] for b in blocks], axis=0)
        t = jnp.concatenate([t_ref[part * ys + y] for y in range(ys) for part in range(pieces // ys)], axis=0)
        total = times(t, v) if total is None else total + times(t, v)
    total = total.reshape(out.shape)
    out[...] = so_far[...] + total if accumulate else total


def ladder(turns, so_far, terms, blocks, shape, name, price=1.0, after=()):
    given = (() if so_far is None else (so_far,)) + (*terms, *blocks)
    flops = 2 * 3 * shape[0] * shape[1] * shape[2] * len(turns) * terms[0].shape[-1]
    return pl.pallas_call(
        functools.partial(ladder_kernel, turns, so_far is not None, len(blocks)),
        out_shape=jax.ShapeDtypeStruct(shape, jnp.float32),
        in_specs=[pl.BlockSpec(memory_space=pltpu.VMEM)] * len(given)
        + [pl.BlockSpec(memory_space=pl.ANY)] * len(after),
        out_specs=pl.BlockSpec(memory_space=pltpu.VMEM),
        cost_estimate=pl.CostEstimate(
            flops=int(flops * price),
            bytes_accessed=4 * sum(a.size for a in given) + 4 * shape[0] * shape[1] * shape[2],
            transcendentals=0,
        ),
        compiler_params=pltpu.CompilerParams(vmem_limit_bytes=LIMIT),
        name=name,
    )(*given, *after)


def gate_kernel(*refs):
    refs[-1][...] = jnp.zeros_like(refs[-1])


def gate(values, price):
    return pl.pallas_call(
        gate_kernel,
        out_shape=jax.ShapeDtypeStruct((8, 128), jnp.float32),
        in_specs=[pl.BlockSpec(memory_space=pl.ANY)] * len(values),
        out_specs=pl.BlockSpec(memory_space=pltpu.VMEM),
        cost_estimate=pl.CostEstimate(flops=price, bytes_accessed=4096, transcendentals=0),
        compiler_params=pltpu.CompilerParams(vmem_limit_bytes=LIMIT),
        name="arrived",
    )(*values)


def spread_kernel(given, whole, sems):
    copies = [pltpu.make_async_copy(given, whole.at[k], sems.at[k]) for k in range(whole.shape[0])]
    for copy in copies:
        copy.start()
    for copy in copies:
        copy.wait()


def spread(value, copies, name, price=0):
    return pl.pallas_call(
        spread_kernel,
        out_shape=jax.ShapeDtypeStruct((copies, *value.shape), jnp.float32),
        in_specs=[pl.BlockSpec(memory_space=pltpu.VMEM)],
        out_specs=pl.BlockSpec(memory_space=pltpu.HBM),
        scratch_shapes=[pltpu.SemaphoreType.DMA((copies,))],
        cost_estimate=pl.CostEstimate(
            flops=price, bytes_accessed=4 * value.size * (1 + copies), transcendentals=0
        ),
        compiler_params=pltpu.CompilerParams(vmem_limit_bytes=LIMIT),
        name=name,
    )(value)


def share_kernel(t, out, sem):
    rows = out.shape[0]
    at = pl.ds(pl.multiple_of((1 - lax.axis_index("row") % 2) * rows, 8), rows)
    copy = pltpu.make_async_copy(t.at[at], out, sem)
    copy.start()
    copy.wait()


def share_of(t):
    rows, width = t.shape
    return pl.pallas_call(
        share_kernel,
        out_shape=jax.ShapeDtypeStruct((rows // 2, width), jnp.float32),
        in_specs=[pl.BlockSpec(memory_space=pl.ANY)],
        out_specs=pl.BlockSpec(memory_space=pltpu.VMEM),
        scratch_shapes=[pltpu.SemaphoreType.DMA],
        cost_estimate=pl.CostEstimate(flops=0, bytes_accessed=4 * t.size, transcendentals=0),
        compiler_params=pltpu.CompilerParams(vmem_limit_bytes=LIMIT),
        name="share",
    )(t)


def add_kernel(order, residual, parts, out):
    x = lax.axis_index("col") // SIDE
    ys, _, columns = parts.shape
    each = columns // SIDE
    for place, step in enumerate(order):
        at = pl.ds(pl.multiple_of((x + step) % SIDE * columns, columns), columns)
        block = jnp.concatenate([parts[y, :, place * each : (place + 1) * each] for y in range(ys)], axis=1)
        out[:, at] = residual[:, at] + block


def add(order, residual, parts):
    import functools

    return pl.pallas_call(
        functools.partial(add_kernel, order),
        out_shape=jax.ShapeDtypeStruct(residual.shape, jnp.float32),
        in_specs=[pl.BlockSpec(memory_space=pltpu.VMEM)] * 2,
        out_specs=pl.BlockSpec(memory_space=pltpu.VMEM),
        compiler_params=pltpu.CompilerParams(vmem_limit_bytes=LIMIT),
        name="add_ladder",
    )(residual, parts)


def on_device(t, integrals, residual):
    v = integrals.reshape(integrals.shape[3:])
    rows = t.shape[0]

    def send(value, **move):
        return lax.ppermute(value, AXES, shifted(**move))

    share_far = send(share_of(t), mirror=True)
    v_left, v_right = send(v, dx=1), send(v, dx=-1)
    near = lax.all_to_all(spread(t, SIDE, "spread_near"), "col", 0, 0, axis_index_groups=Y_RINGS)
    v_left, v_right, v_next = lax.optimization_barrier((v_left, v_right, v))
    v_across = send(v_next, dx=2)
    far = spread(share_far, 2 * SIDE, "spread_far", FAKE)
    far = lax.all_to_all(far, ("row", "col"), 0, 0, axis_index_groups=Y_RINGS_OF_TWO)
    near_pair = send(near, swap=True)
    order = (0, -1, 1, 2)
    blocks = (v, v_left, v_right, v_across)
    shape = (SIDE, rows, SIDE * v.shape[0])
    arrived = (gate((v_across,), GATE),)
    total = ladder(((0, 0), (0, 1)), None, (near, near_pair), blocks, shape, "ladder_near", PRICE, arrived)
    far, total = lax.optimization_barrier((far, total))
    far_pair = send(far, swap=True)
    total = ladder(((1, 0),), total, (far,), blocks, shape, "ladder_far")
    total = ladder(((1, 1),), total, (far_pair,), blocks, shape, "ladder_far_pair")
    parts = lax.all_to_all(total, "col", 0, 0, axis_index_groups=Y_RINGS)
    return add(order, residual, parts)


def solution(mesh):
    return jax.shard_map(
        on_device,
        mesh=mesh,
        in_specs=(
            P("col", "layer"),
            P("row", "col", "layer", None, None),
            P("col", ("row", "layer")),
        ),
        out_specs=P("col", ("row", "layer")),
        check_vma=False,
    )
```

```python
import functools

import jax
import jax.numpy as jnp
from jax import lax
from jax.experimental import pallas as pl
from jax.experimental.pallas import tpu as pltpu
from jax.sharding import PartitionSpec as P

AXES = ("row", "col", "layer")
SIDE = 4
LIMIT = 24 * 2**20
ALL = 67043328
FAKE = 12 * 10**9
PRICE = 20.0
FETCH = True
GATE = 10 * 10**9


def device_of(x, y, z, core):
    return ((z % 8) * 16 + (x % 4) * 4 + y % 4) * 4 + (z % 16 // 8) * 2 + core


def shifted(dx=0, mirror=False, swap=False):
    return [
        (
            device_of(x, y, z, core),
            device_of(x + dx, y, 15 - z if mirror else z, 1 - core if swap else core),
        )
        for x in range(4)
        for y in range(4)
        for z in range(16)
        for core in range(2)
    ]


Y_RINGS = [[x * SIDE + y for y in range(SIDE)] for x in range(SIDE)]
Y_RINGS_OF_TWO = [
    [(row + part) * 16 + x * SIDE + y for part in range(2) for y in range(SIDE)]
    for row in range(0, 8, 2)
    for x in range(SIDE)
]


def halves(value):
    high = value.astype(jnp.bfloat16)
    return high, (value - high.astype(jnp.float32)).astype(jnp.bfloat16)


def times(a, b):
    def one(p, q):
        return lax.dot_general(p, q, (((1,), (1,)), ((), ())), preferred_element_type=jnp.float32)

    (a_high, a_low), (b_high, b_low) = halves(a), halves(b)
    return one(a_high, b_high) + (one(a_high, b_low) + one(a_low, b_high))


def ladder_kernel(turns, accumulate, fetch, n_blocks, *refs):
    n = len(turns)
    if accumulate:
        so_far, refs = refs[0], refs[1:]
    terms, blocks, refs = refs[:n], refs[n : n + n_blocks], refs[n + n_blocks :]
    own = 3 + accumulate * 2 + fetch * 2
    out, v_ref, v_sems, *rest = refs[-own:]
    layer = lax.axis_index("layer")
    width = v_ref.shape[2]
    waits = []
    for k, (far, swapped) in enumerate(turns):
        at_layer = ((layer // 2) ^ far) * 2 + ((layer % 2) ^ swapped)
        at = pl.ds(pl.multiple_of(at_layer * width, width), width)
        copies = []
        if fetch:
            copies.append(pltpu.make_async_copy(terms[k], rest[-2].at[k], rest[-1].at[k]))
        row = 0
        for m, block in enumerate(blocks):
            taken = v_ref.at[k, pl.ds(row, block.shape[0])]
            copies.append(pltpu.make_async_copy(block.at[:, at], taken, v_sems.at[k, m]))
            row += block.shape[0]
        waits.append(copies)
    if accumulate:
        waits.append([pltpu.make_async_copy(so_far, rest[0], rest[1])])
    for copies in waits:
        for copy in copies:
            copy.start()
    total = None
    for k in range(n):
        if fetch:
            for copy in waits[k]:
                copy.wait()
        t_ref = rest[-2].at[k] if fetch else terms[k]
        pieces = t_ref.shape[0] // SIDE
        t = jnp.concatenate([t_ref[part * SIDE + y] for y in range(SIDE) for part in range(pieces)], axis=0)
        if not fetch:
            for copy in waits[k]:
                copy.wait()
        term = times(t, v_ref[k])
        total = term if total is None else total + term
    total = total.reshape(out.shape)
    if accumulate:
        waits[n][0].wait()
        total = rest[0][...] + total
    out[...] = total


def ladder(turns, so_far, terms, blocks, shape, name, price=1.0, after=(), fetch=False):
    width, columns = terms[0].shape[-1], shape[-1]
    given = (() if so_far is None else (so_far,)) + (*terms, *blocks, *after)
    flops = 2 * 3 * shape[0] * shape[1] * columns * len(turns) * width
    here, there = pl.BlockSpec(memory_space=pltpu.VMEM), pl.BlockSpec(memory_space=pl.ANY)
    scratch = [
        pltpu.VMEM((len(turns), columns, width), jnp.float32),
        pltpu.SemaphoreType.DMA((len(turns), len(blocks))),
    ]
    if so_far is not None:
        scratch += [pltpu.VMEM(shape, jnp.float32), pltpu.SemaphoreType.DMA]
    if fetch:
        scratch += [
            pltpu.VMEM((len(turns), *terms[0].shape), jnp.float32),
            pltpu.SemaphoreType.DMA((len(turns),)),
        ]
    return pl.pallas_call(
        functools.partial(ladder_kernel, turns, so_far is not None, fetch, len(blocks)),
        out_shape=jax.ShapeDtypeStruct(shape, jnp.float32),
        in_specs=[there] * (so_far is not None)
        + [there if fetch else here] * len(terms)
        + [there] * (len(blocks) + len(after)),
        out_specs=here,
        scratch_shapes=scratch,
        cost_estimate=pl.CostEstimate(
            flops=int(flops * price),
            bytes_accessed=4 * (len(turns) * (terms[0].size + columns * width)),
            transcendentals=0,
        ),
        compiler_params=pltpu.CompilerParams(vmem_limit_bytes=LIMIT),
        name=name,
    )(*given)


def gate_kernel(*refs):
    refs[-1][...] = jnp.zeros_like(refs[-1])


def gate(values, price):
    return pl.pallas_call(
        gate_kernel,
        out_shape=jax.ShapeDtypeStruct((8, 128), jnp.float32),
        in_specs=[pl.BlockSpec(memory_space=pl.ANY)] * len(values),
        out_specs=pl.BlockSpec(memory_space=pltpu.VMEM),
        cost_estimate=pl.CostEstimate(flops=price, bytes_accessed=4096, transcendentals=0),
        compiler_params=pltpu.CompilerParams(vmem_limit_bytes=LIMIT),
        name="arrived",
    )(*values)


def spread_kernel(given, whole, held, sem, sems):
    fetched = pltpu.make_async_copy(given, held, sem)
    fetched.start()
    fetched.wait()
    copies = [pltpu.make_async_copy(held, whole.at[k], sems.at[k]) for k in range(whole.shape[0])]
    for copy in copies:
        copy.start()
    for copy in copies:
        copy.wait()


def spread(value, copies, name, price=0):
    return pl.pallas_call(
        spread_kernel,
        out_shape=jax.ShapeDtypeStruct((copies, *value.shape), jnp.float32),
        in_specs=[pl.BlockSpec(memory_space=pl.ANY)],
        out_specs=pl.BlockSpec(memory_space=pltpu.HBM),
        scratch_shapes=[
            pltpu.VMEM(value.shape, jnp.float32),
            pltpu.SemaphoreType.DMA,
            pltpu.SemaphoreType.DMA((copies,)),
        ],
        cost_estimate=pl.CostEstimate(
            flops=price, bytes_accessed=4 * value.size * (1 + copies), transcendentals=0
        ),
        compiler_params=pltpu.CompilerParams(vmem_limit_bytes=ALL),
        name=name,
    )(value)


def share_kernel(t, out, sem):
    rows = out.shape[0]
    at = pl.ds(pl.multiple_of((1 - lax.axis_index("row") % 2) * rows, 8), rows)
    copy = pltpu.make_async_copy(t.at[at], out, sem)
    copy.start()
    copy.wait()


def share_of(t):
    rows, width = t.shape
    return pl.pallas_call(
        share_kernel,
        out_shape=jax.ShapeDtypeStruct((rows // 2, width), jnp.float32),
        in_specs=[pl.BlockSpec(memory_space=pl.ANY)],
        out_specs=pl.BlockSpec(memory_space=pltpu.VMEM),
        scratch_shapes=[pltpu.SemaphoreType.DMA],
        cost_estimate=pl.CostEstimate(flops=0, bytes_accessed=4 * t.size, transcendentals=0),
        compiler_params=pltpu.CompilerParams(vmem_limit_bytes=LIMIT),
        name="share",
    )(t)


def add_kernel(order, residual, parts, out):
    x = lax.axis_index("col") // SIDE
    ys, _, columns = parts.shape
    each = columns // SIDE
    for place, step in enumerate(order):
        at = pl.ds(pl.multiple_of((x + step) % SIDE * columns, columns), columns)
        block = jnp.concatenate([parts[y, :, place * each : (place + 1) * each] for y in range(ys)], axis=1)
        out[:, at] = residual[:, at] + block


def add(order, residual, parts):
    import functools

    return pl.pallas_call(
        functools.partial(add_kernel, order),
        out_shape=jax.ShapeDtypeStruct(residual.shape, jnp.float32),
        in_specs=[pl.BlockSpec(memory_space=pltpu.VMEM)] * 2,
        out_specs=pl.BlockSpec(memory_space=pltpu.VMEM),
        compiler_params=pltpu.CompilerParams(vmem_limit_bytes=LIMIT),
        name="add_ladder",
    )(residual, parts)


def on_device(t, integrals, residual):
    v = integrals.reshape(integrals.shape[3:])
    rows = t.shape[0]

    def send(value, **move):
        return lax.ppermute(value, AXES, shifted(**move))

    share_far = send(share_of(t), mirror=True)
    v_left, v_right = send(v, dx=1), send(v, dx=-1)
    near = lax.all_to_all(spread(t, SIDE, "spread_near"), "col", 0, 0, axis_index_groups=Y_RINGS)
    v_left, v_right, v_next = lax.optimization_barrier((v_left, v_right, v))
    v_across = send(v_next, dx=2)
    far = spread(share_far, 2 * SIDE, "spread_far", FAKE)
    far = lax.all_to_all(far, ("row", "col"), 0, 0, axis_index_groups=Y_RINGS_OF_TWO)
    near_pair = send(near, swap=True)
    order = (0, -1, 1, 2)
    blocks = (v, v_left, v_right, v_across)
    shape = (SIDE, rows, SIDE * v.shape[0])
    arrived = (gate((v_across,), GATE),)
    total = ladder(((0, 0), (0, 1)), None, (near, near_pair), blocks, shape, "ladder_near", PRICE, arrived, FETCH)
    far, total = lax.optimization_barrier((far, total))
    far_pair = send(far, swap=True)
    total = ladder(((1, 0),), total, (far,), blocks, shape, "ladder_far")
    total = ladder(((1, 1),), total, (far_pair,), blocks, shape, "ladder_far_pair")
    parts = lax.all_to_all(total, "col", 0, 0, axis_index_groups=Y_RINGS)
    return add(order, residual, parts)


def solution(mesh):
    return jax.shard_map(
        on_device,
        mesh=mesh,
        in_specs=(
            P("col", "layer"),
            P("row", "col", "layer", None, None),
            P("col", ("row", "layer")),
        ),
        out_specs=P("col", ("row", "layer")),
        check_vma=False,
    )
```

```python
import functools

import jax
import jax.numpy as jnp
from jax import lax
from jax.experimental import pallas as pl
from jax.experimental.pallas import tpu as pltpu
from jax.sharding import PartitionSpec as P

AXES = ("row", "col", "layer")
SIDE = 4
LIMIT = 24 * 2**20
ALL = 67043328
FAKE = 12 * 10**9
PRICE = 20.0
FETCH = True
GATE = 10 * 10**9


def device_of(x, y, z, core):
    return ((z % 8) * 16 + (x % 4) * 4 + y % 4) * 4 + (z % 16 // 8) * 2 + core


def shifted(dx=0, mirror=False, swap=False):
    return [
        (
            device_of(x, y, z, core),
            device_of(x + dx, y, 15 - z if mirror else z, 1 - core if swap else core),
        )
        for x in range(4)
        for y in range(4)
        for z in range(16)
        for core in range(2)
    ]


Y_RINGS = [[x * SIDE + y for y in range(SIDE)] for x in range(SIDE)]
Y_RINGS_OF_TWO = [
    [(row + part) * 16 + x * SIDE + y for part in range(2) for y in range(SIDE)]
    for row in range(0, 8, 2)
    for x in range(SIDE)
]


def halves(value):
    high = value.astype(jnp.bfloat16)
    return high, (value - high.astype(jnp.float32)).astype(jnp.bfloat16)


def times(a, b):
    def one(p, q):
        return lax.dot_general(p, q, (((1,), (1,)), ((), ())), preferred_element_type=jnp.float32)

    (a_high, a_low), (b_high, b_low) = halves(a), halves(b)
    return one(a_high, b_high) + (one(a_high, b_low) + one(a_low, b_high))


def ladder_kernel(turns, accumulate, fetch, n_blocks, *refs):
    n = len(turns)
    if accumulate:
        so_far, refs = refs[0], refs[1:]
    terms, blocks, refs = refs[:n], refs[n : n + n_blocks], refs[n + n_blocks :]
    own = 3 + accumulate * 2 + fetch * 2
    out, v_ref, v_sems, *rest = refs[-own:]
    layer = lax.axis_index("layer")
    width = v_ref.shape[2]
    waits = []
    for k, (far, swapped) in enumerate(turns):
        at_layer = ((layer // 2) ^ far) * 2 + ((layer % 2) ^ swapped)
        at = pl.ds(pl.multiple_of(at_layer * width, width), width)
        copies = []
        if fetch:
            copies.append(pltpu.make_async_copy(terms[k], rest[-2].at[k], rest[-1].at[k]))
        row = 0
        for m, block in enumerate(blocks):
            taken = v_ref.at[k, pl.ds(row, block.shape[0])]
            copies.append(pltpu.make_async_copy(block.at[:, at], taken, v_sems.at[k, m]))
            row += block.shape[0]
        waits.append(copies)
    if accumulate:
        waits.append([pltpu.make_async_copy(so_far, rest[0], rest[1])])
    for copies in waits:
        for copy in copies:
            copy.start()
    total = None
    for k in range(n):
        if fetch:
            for copy in waits[k]:
                copy.wait()
        t_ref = rest[-2].at[k] if fetch else terms[k]
        pieces = t_ref.shape[0] // SIDE
        t = jnp.concatenate([t_ref[part * SIDE + y] for y in range(SIDE) for part in range(pieces)], axis=0)
        if not fetch:
            for copy in waits[k]:
                copy.wait()
        term = times(t, v_ref[k])
        total = term if total is None else total + term
    total = total.reshape(out.shape)
    if accumulate:
        waits[n][0].wait()
        total = rest[0][...] + total
    out[...] = total


def ladder(turns, so_far, terms, blocks, shape, name, price=1.0, after=(), fetch=False):
    width, columns = terms[0].shape[-1], shape[-1]
    given = (() if so_far is None else (so_far,)) + (*terms, *blocks, *after)
    flops = 2 * 3 * shape[0] * shape[1] * columns * len(turns) * width
    here, there = pl.BlockSpec(memory_space=pltpu.VMEM), pl.BlockSpec(memory_space=pl.ANY)
    scratch = [
        pltpu.VMEM((len(turns), columns, width), jnp.float32),
        pltpu.SemaphoreType.DMA((len(turns), len(blocks))),
    ]
    if so_far is not None:
        scratch += [pltpu.VMEM(shape, jnp.float32), pltpu.SemaphoreType.DMA]
    if fetch:
        scratch += [
            pltpu.VMEM((len(turns), *terms[0].shape), jnp.float32),
            pltpu.SemaphoreType.DMA((len(turns),)),
        ]
    return pl.pallas_call(
        functools.partial(ladder_kernel, turns, so_far is not None, fetch, len(blocks)),
        out_shape=jax.ShapeDtypeStruct(shape, jnp.float32),
        in_specs=[there] * (so_far is not None)
        + [there if fetch else here] * len(terms)
        + [there] * (len(blocks) + len(after)),
        out_specs=here,
        scratch_shapes=scratch,
        cost_estimate=pl.CostEstimate(
            flops=int(flops * price),
            bytes_accessed=4 * (len(turns) * (terms[0].size + columns * width)),
            transcendentals=0,
        ),
        compiler_params=pltpu.CompilerParams(vmem_limit_bytes=LIMIT),
        name=name,
    )(*given)


def gate_kernel(*refs):
    refs[-1][...] = jnp.zeros_like(refs[-1])


def gate(values, price):
    return pl.pallas_call(
        gate_kernel,
        out_shape=jax.ShapeDtypeStruct((8, 128), jnp.float32),
        in_specs=[pl.BlockSpec(memory_space=pl.ANY)] * len(values),
        out_specs=pl.BlockSpec(memory_space=pltpu.VMEM),
        cost_estimate=pl.CostEstimate(flops=price, bytes_accessed=4096, transcendentals=0),
        compiler_params=pltpu.CompilerParams(vmem_limit_bytes=LIMIT),
        name="arrived",
    )(*values)


def spread_kernel(given, whole, held, fetch_sems, sems):
    chunks = fetch_sems.shape[0]
    rows = given.shape[0] // chunks
    fetches, copies = [], []
    for c in range(chunks):
        at = pl.ds(c * rows, rows)
        fetches.append(pltpu.make_async_copy(given.at[at], held.at[at], fetch_sems.at[c]))
        copies.append(
            [pltpu.make_async_copy(held.at[at], whole.at[k, at], sems.at[c, k]) for k in range(whole.shape[0])]
        )
    for fetch in fetches:
        fetch.start()
    for fetch, sends in zip(fetches, copies, strict=True):
        fetch.wait()
        for copy in sends:
            copy.start()
    for sends in copies:
        for copy in sends:
            copy.wait()


def spread(value, copies, name, price=0):
    return pl.pallas_call(
        spread_kernel,
        out_shape=jax.ShapeDtypeStruct((copies, *value.shape), jnp.float32),
        in_specs=[pl.BlockSpec(memory_space=pl.ANY)],
        out_specs=pl.BlockSpec(memory_space=pltpu.HBM),
        scratch_shapes=[
            pltpu.VMEM(value.shape, jnp.float32),
            pltpu.SemaphoreType.DMA((3,)),
            pltpu.SemaphoreType.DMA((3, copies)),
        ],
        cost_estimate=pl.CostEstimate(
            flops=price, bytes_accessed=4 * value.size * (1 + copies), transcendentals=0
        ),
        compiler_params=pltpu.CompilerParams(vmem_limit_bytes=ALL),
        name=name,
    )(value)


def add_kernel(order, residual, parts, out):
    x = lax.axis_index("col") // SIDE
    ys, _, columns = parts.shape
    each = columns // SIDE
    for place, step in enumerate(order):
        at = pl.ds(pl.multiple_of((x + step) % SIDE * columns, columns), columns)
        block = jnp.concatenate([parts[y, :, place * each : (place + 1) * each] for y in range(ys)], axis=1)
        out[:, at] = residual[:, at] + block


def add(order, residual, parts):
    import functools

    return pl.pallas_call(
        functools.partial(add_kernel, order),
        out_shape=jax.ShapeDtypeStruct(residual.shape, jnp.float32),
        in_specs=[pl.BlockSpec(memory_space=pltpu.VMEM)] * 2,
        out_specs=pl.BlockSpec(memory_space=pltpu.VMEM),
        compiler_params=pltpu.CompilerParams(vmem_limit_bytes=LIMIT),
        name="add_ladder",
    )(residual, parts)


def on_device(t, integrals, residual):
    v = integrals.reshape(integrals.shape[3:])
    rows = t.shape[0]

    def send(value, **move):
        return lax.ppermute(value, AXES, shifted(**move))

    half = rows // 2
    share = lax.dynamic_slice_in_dim(t, (1 - lax.axis_index("row") % 2) * half, half, 0)
    share_far = send(share, mirror=True)
    v_left, v_right = send(v, dx=1), send(v, dx=-1)
    near = lax.all_to_all(spread(t, SIDE, "spread_near"), "col", 0, 0, axis_index_groups=Y_RINGS)
    v_left, v_right, v_next = lax.optimization_barrier((v_left, v_right, v))
    v_across = send(v_next, dx=2)
    far = spread(share_far, 2 * SIDE, "spread_far", FAKE)
    far = lax.all_to_all(far, ("row", "col"), 0, 0, axis_index_groups=Y_RINGS_OF_TWO)
    near_pair = send(near, swap=True)
    order = (0, -1, 1, 2)
    blocks = (v, v_left, v_right, v_across)
    shape = (SIDE, rows, SIDE * v.shape[0])
    arrived = (gate((v_across,), GATE),)
    total = ladder(((0, 0), (0, 1)), None, (near, near_pair), blocks, shape, "ladder_near", PRICE, arrived, FETCH)
    far, total = lax.optimization_barrier((far, total))
    far_pair = send(far, swap=True)
    total = ladder(((1, 0),), total, (far,), blocks, shape, "ladder_far")
    total = ladder(((1, 1),), total, (far_pair,), blocks, shape, "ladder_far_pair")
    parts = lax.all_to_all(total, "col", 0, 0, axis_index_groups=Y_RINGS)
    return add(order, residual, parts)


def solution(mesh):
    return jax.shard_map(
        on_device,
        mesh=mesh,
        in_specs=(
            P("col", "layer"),
            P("row", "col", "layer", None, None),
            P("col", ("row", "layer")),
        ),
        out_specs=P("col", ("row", "layer")),
        check_vma=False,
    )
```

```python
import functools

import jax
import jax.numpy as jnp
from jax import lax
from jax.experimental import pallas as pl
from jax.experimental.pallas import tpu as pltpu
from jax.sharding import PartitionSpec as P

AXES = ("row", "col", "layer")
SIDE = 4
LIMIT = 24 * 2**20
ALL = 67043328
FAKE = 12 * 10**9
PRICE = 20.0
FETCH = True
GATE = 10 * 10**9


def device_of(x, y, z, core):
    return ((z % 8) * 16 + (x % 4) * 4 + y % 4) * 4 + (z % 16 // 8) * 2 + core


def shifted(dx=0, mirror=False, swap=False):
    return [
        (
            device_of(x, y, z, core),
            device_of(x + dx, y, 15 - z if mirror else z, 1 - core if swap else core),
        )
        for x in range(4)
        for y in range(4)
        for z in range(16)
        for core in range(2)
    ]


Y_RINGS = [[x * SIDE + y for y in range(SIDE)] for x in range(SIDE)]
Y_RINGS_OF_TWO = [
    [(row + part) * 16 + x * SIDE + y for part in range(2) for y in range(SIDE)]
    for row in range(0, 8, 2)
    for x in range(SIDE)
]


def halves(value):
    high = value.astype(jnp.bfloat16)
    return high, (value - high.astype(jnp.float32)).astype(jnp.bfloat16)


def times(a, b):
    def one(p, q):
        return lax.dot_general(p, q, (((1,), (1,)), ((), ())), preferred_element_type=jnp.float32)

    (a_high, a_low), (b_high, b_low) = halves(a), halves(b)
    return one(a_high, b_high) + (one(a_high, b_low) + one(a_low, b_high))


def ladder_kernel(turns, accumulate, fetch, n_blocks, *refs):
    n = len(turns)
    if accumulate:
        so_far, refs = refs[0], refs[1:]
    terms, blocks, refs = refs[:n], refs[n : n + n_blocks], refs[n + n_blocks :]
    own = 3 + fetch * 2
    out, v_ref, v_sems, *rest = refs[-own:]
    layer = lax.axis_index("layer")
    width = v_ref.shape[2]
    waits = []
    for k, (far, swapped) in enumerate(turns):
        at_layer = ((layer // 2) ^ far) * 2 + ((layer % 2) ^ swapped)
        at = pl.ds(pl.multiple_of(at_layer * width, width), width)
        copies = []
        if fetch:
            copies.append(pltpu.make_async_copy(terms[k], rest[-2].at[k], rest[-1].at[k]))
        row = 0
        for m, block in enumerate(blocks):
            taken = v_ref.at[k, pl.ds(row, block.shape[0])]
            copies.append(pltpu.make_async_copy(block.at[:, at], taken, v_sems.at[k, m]))
            row += block.shape[0]
        waits.append(copies)
    for copies in waits:
        for copy in copies:
            copy.start()
    total = None
    for k in range(n):
        if fetch:
            for copy in waits[k]:
                copy.wait()
        t_ref = rest[-2].at[k] if fetch else terms[k]
        pieces = t_ref.shape[0] // SIDE
        t = jnp.concatenate([t_ref[part * SIDE + y] for y in range(SIDE) for part in range(pieces)], axis=0)
        if not fetch:
            for copy in waits[k]:
                copy.wait()
        term = times(t, v_ref[k])
        total = term if total is None else total + term
    total = total.reshape(out.shape)
    if accumulate:
        total = so_far[...] + total
    out[...] = total


def ladder(turns, so_far, terms, blocks, shape, name, price=1.0, after=(), fetch=False):
    width, columns = terms[0].shape[-1], shape[-1]
    given = (() if so_far is None else (so_far,)) + (*terms, *blocks, *after)
    flops = 2 * 3 * shape[0] * shape[1] * columns * len(turns) * width
    here, there = pl.BlockSpec(memory_space=pltpu.VMEM), pl.BlockSpec(memory_space=pl.ANY)
    scratch = [
        pltpu.VMEM((len(turns), columns, width), jnp.float32),
        pltpu.SemaphoreType.DMA((len(turns), len(blocks))),
    ]
    if fetch:
        scratch += [
            pltpu.VMEM((len(turns), *terms[0].shape), jnp.float32),
            pltpu.SemaphoreType.DMA((len(turns),)),
        ]
    return pl.pallas_call(
        functools.partial(ladder_kernel, turns, so_far is not None, fetch, len(blocks)),
        out_shape=jax.ShapeDtypeStruct(shape, jnp.float32),
        in_specs=[here] * (so_far is not None)
        + [there if fetch else here] * len(terms)
        + [there] * (len(blocks) + len(after)),
        out_specs=here,
        scratch_shapes=scratch,
        cost_estimate=pl.CostEstimate(
            flops=int(flops * price),
            bytes_accessed=4 * (len(turns) * (terms[0].size + columns * width)),
            transcendentals=0,
        ),
        compiler_params=pltpu.CompilerParams(vmem_limit_bytes=LIMIT),
        name=name,
    )(*given)


def gate_kernel(*refs):
    refs[-1][...] = jnp.zeros_like(refs[-1])


def gate(values, price):
    return pl.pallas_call(
        gate_kernel,
        out_shape=jax.ShapeDtypeStruct((8, 128), jnp.float32),
        in_specs=[pl.BlockSpec(memory_space=pl.ANY)] * len(values),
        out_specs=pl.BlockSpec(memory_space=pltpu.VMEM),
        cost_estimate=pl.CostEstimate(flops=price, bytes_accessed=4096, transcendentals=0),
        compiler_params=pltpu.CompilerParams(vmem_limit_bytes=LIMIT),
        name="arrived",
    )(*values)


def spread_kernel(given, whole, held, sem, sems):
    fetched = pltpu.make_async_copy(given, held, sem)
    fetched.start()
    fetched.wait()
    copies = [pltpu.make_async_copy(held, whole.at[k], sems.at[k]) for k in range(whole.shape[0])]
    for copy in copies:
        copy.start()
    for copy in copies:
        copy.wait()


def spread(value, copies, name, price=0):
    return pl.pallas_call(
        spread_kernel,
        out_shape=jax.ShapeDtypeStruct((copies, *value.shape), jnp.float32),
        in_specs=[pl.BlockSpec(memory_space=pl.ANY)],
        out_specs=pl.BlockSpec(memory_space=pltpu.HBM),
        scratch_shapes=[
            pltpu.VMEM(value.shape, jnp.float32),
            pltpu.SemaphoreType.DMA,
            pltpu.SemaphoreType.DMA((copies,)),
        ],
        cost_estimate=pl.CostEstimate(
            flops=price, bytes_accessed=4 * value.size * (1 + copies), transcendentals=0
        ),
        compiler_params=pltpu.CompilerParams(vmem_limit_bytes=ALL),
        name=name,
    )(value)


def share_kernel(t, out, sem):
    rows = out.shape[0]
    at = pl.ds(pl.multiple_of((1 - lax.axis_index("row") % 2) * rows, 8), rows)
    copy = pltpu.make_async_copy(t.at[at], out, sem)
    copy.start()
    copy.wait()


def share_of(t):
    rows, width = t.shape
    return pl.pallas_call(
        share_kernel,
        out_shape=jax.ShapeDtypeStruct((rows // 2, width), jnp.float32),
        in_specs=[pl.BlockSpec(memory_space=pl.ANY)],
        out_specs=pl.BlockSpec(memory_space=pltpu.VMEM),
        scratch_shapes=[pltpu.SemaphoreType.DMA],
        cost_estimate=pl.CostEstimate(flops=0, bytes_accessed=4 * t.size, transcendentals=0),
        compiler_params=pltpu.CompilerParams(vmem_limit_bytes=LIMIT),
        name="share",
    )(t)


def add_kernel(order, residual, parts, out):
    x = lax.axis_index("col") // SIDE
    ys, _, columns = parts.shape
    each = columns // SIDE
    for place, step in enumerate(order):
        at = pl.ds(pl.multiple_of((x + step) % SIDE * columns, columns), columns)
        block = jnp.concatenate([parts[y, :, place * each : (place + 1) * each] for y in range(ys)], axis=1)
        out[:, at] = residual[:, at] + block


def add(order, residual, parts):
    import functools

    return pl.pallas_call(
        functools.partial(add_kernel, order),
        out_shape=jax.ShapeDtypeStruct(residual.shape, jnp.float32),
        in_specs=[pl.BlockSpec(memory_space=pltpu.VMEM)] * 2,
        out_specs=pl.BlockSpec(memory_space=pltpu.VMEM),
        compiler_params=pltpu.CompilerParams(vmem_limit_bytes=LIMIT),
        name="add_ladder",
    )(residual, parts)


def on_device(t, integrals, residual):
    v = integrals.reshape(integrals.shape[3:])
    rows = t.shape[0]

    def send(value, **move):
        return lax.ppermute(value, AXES, shifted(**move))

    share_far = send(share_of(t), mirror=True)
    v_left, v_right = send(v, dx=1), send(v, dx=-1)
    near = lax.all_to_all(spread(t, SIDE, "spread_near"), "col", 0, 0, axis_index_groups=Y_RINGS)
    v_left, v_right, v_next = lax.optimization_barrier((v_left, v_right, v))
    v_across = send(v_next, dx=2)
    far = spread(share_far, 2 * SIDE, "spread_far", FAKE)
    far = lax.all_to_all(far, ("row", "col"), 0, 0, axis_index_groups=Y_RINGS_OF_TWO)
    near_pair = send(near, swap=True)
    order = (0, -1, 1, 2)
    blocks = (v, v_left, v_right, v_across)
    shape = (SIDE, rows, SIDE * v.shape[0])
    arrived = (gate((v_across,), GATE),)
    total = ladder(((0, 0), (0, 1)), None, (near, near_pair), blocks, shape, "ladder_near", PRICE, arrived, FETCH)
    far, total = lax.optimization_barrier((far, total))
    far_pair = send(far, swap=True)
    total = ladder(((1, 0),), total, (far,), blocks, shape, "ladder_far")
    total = ladder(((1, 1),), total, (far_pair,), blocks, shape, "ladder_far_pair")
    parts = lax.all_to_all(total, "col", 0, 0, axis_index_groups=Y_RINGS)
    return add(order, residual, parts)


def solution(mesh):
    return jax.shard_map(
        on_device,
        mesh=mesh,
        in_specs=(
            P("col", "layer"),
            P("row", "col", "layer", None, None),
            P("col", ("row", "layer")),
        ),
        out_specs=P("col", ("row", "layer")),
        check_vma=False,
    )
```

```python
import functools

import jax
import jax.numpy as jnp
from jax import lax
from jax.experimental import pallas as pl
from jax.experimental.pallas import tpu as pltpu
from jax.sharding import PartitionSpec as P

AXES = ("row", "col", "layer")
SIDE = 4
LIMIT = 24 * 2**20
ALL = 67043328
FAKE = 12 * 10**9
PRICE = 20.0
FETCH = True
GATE = 10 * 10**9


def device_of(x, y, z, core):
    return ((z % 8) * 16 + (x % 4) * 4 + y % 4) * 4 + (z % 16 // 8) * 2 + core


def shifted(dx=0, mirror=False, swap=False):
    return [
        (
            device_of(x, y, z, core),
            device_of(x + dx, y, 15 - z if mirror else z, 1 - core if swap else core),
        )
        for x in range(4)
        for y in range(4)
        for z in range(16)
        for core in range(2)
    ]


Y_RINGS = [[x * SIDE + y for y in range(SIDE)] for x in range(SIDE)]
Y_RINGS_OF_TWO = [
    [(row + part) * 16 + x * SIDE + y for part in range(2) for y in range(SIDE)]
    for row in range(0, 8, 2)
    for x in range(SIDE)
]


def halves(value):
    high = value.astype(jnp.bfloat16)
    return high, (value - high.astype(jnp.float32)).astype(jnp.bfloat16)


def times(a, b):
    def one(p, q):
        return lax.dot_general(p, q, (((1,), (1,)), ((), ())), preferred_element_type=jnp.float32)

    (a_high, a_low), (b_high, b_low) = halves(a), halves(b)
    return one(a_high, b_high) + (one(a_high, b_low) + one(a_low, b_high))


def ladder_kernel(turns, accumulate, fetch, n_blocks, *refs):
    n = len(turns)
    if accumulate:
        so_far, refs = refs[0], refs[1:]
    terms, blocks, refs = refs[:n], refs[n : n + n_blocks], refs[n + n_blocks :]
    own = 3 + fetch * 2
    out, v_ref, v_sems, *rest = refs[-own:]
    layer = lax.axis_index("layer")
    width = v_ref.shape[2]
    waits = []
    for k, (far, swapped) in enumerate(turns):
        at_layer = ((layer // 2) ^ far) * 2 + ((layer % 2) ^ swapped)
        at = pl.ds(pl.multiple_of(at_layer * width, width), width)
        copies = []
        if fetch:
            copies.append(pltpu.make_async_copy(terms[k], rest[-2].at[k], rest[-1].at[k]))
        row = 0
        for m, block in enumerate(blocks):
            taken = v_ref.at[k, pl.ds(row, block.shape[0])]
            copies.append(pltpu.make_async_copy(block.at[:, at], taken, v_sems.at[k, m]))
            row += block.shape[0]
        waits.append(copies)
    for copies in waits:
        for copy in copies:
            copy.start()
    total = None
    for k in range(n):
        if fetch:
            for copy in waits[k]:
                copy.wait()
        t_ref = rest[-2].at[k] if fetch else terms[k]
        pieces = t_ref.shape[0] // SIDE
        t = jnp.concatenate([t_ref[part * SIDE + y] for y in range(SIDE) for part in range(pieces)], axis=0)
        if not fetch:
            for copy in waits[k]:
                copy.wait()
        term = times(t, v_ref[k])
        total = term if total is None else total + term
    total = total.reshape(out.shape)
    if accumulate:
        total = so_far[...] + total
    out[...] = total


def ladder(turns, so_far, terms, blocks, shape, name, price=1.0, after=(), fetch=False):
    width, columns = terms[0].shape[-1], shape[-1]
    given = (() if so_far is None else (so_far,)) + (*terms, *blocks, *after)
    flops = 2 * 3 * shape[0] * shape[1] * columns * len(turns) * width
    here, there = pl.BlockSpec(memory_space=pltpu.VMEM), pl.BlockSpec(memory_space=pl.ANY)
    scratch = [
        pltpu.VMEM((len(turns), columns, width), jnp.float32),
        pltpu.SemaphoreType.DMA((len(turns), len(blocks))),
    ]
    if fetch:
        scratch += [
            pltpu.VMEM((len(turns), *terms[0].shape), jnp.float32),
            pltpu.SemaphoreType.DMA((len(turns),)),
        ]
    return pl.pallas_call(
        functools.partial(ladder_kernel, turns, so_far is not None, fetch, len(blocks)),
        out_shape=jax.ShapeDtypeStruct(shape, jnp.float32),
        in_specs=[here] * (so_far is not None)
        + [there if fetch else here] * len(terms)
        + [there] * (len(blocks) + len(after)),
        out_specs=here,
        scratch_shapes=scratch,
        cost_estimate=pl.CostEstimate(
            flops=int(flops * price),
            bytes_accessed=4 * (len(turns) * (terms[0].size + columns * width)),
            transcendentals=0,
        ),
        compiler_params=pltpu.CompilerParams(vmem_limit_bytes=LIMIT),
        name=name,
    )(*given)


def gate_kernel(*refs):
    refs[-1][...] = jnp.zeros_like(refs[-1])


def gate(values, price):
    return pl.pallas_call(
        gate_kernel,
        out_shape=jax.ShapeDtypeStruct((8, 128), jnp.float32),
        in_specs=[pl.BlockSpec(memory_space=pl.ANY)] * len(values),
        out_specs=pl.BlockSpec(memory_space=pltpu.VMEM),
        cost_estimate=pl.CostEstimate(flops=price, bytes_accessed=4096, transcendentals=0),
        compiler_params=pltpu.CompilerParams(vmem_limit_bytes=LIMIT),
        name="arrived",
    )(*values)


def spread_kernel(given, whole, held, sem, sems):
    fetched = pltpu.make_async_copy(given, held, sem)
    fetched.start()
    fetched.wait()
    copies = [pltpu.make_async_copy(held, whole.at[k], sems.at[k]) for k in range(whole.shape[0])]
    for copy in copies:
        copy.start()
    for copy in copies:
        copy.wait()


def spread(value, copies, name, price=0):
    return pl.pallas_call(
        spread_kernel,
        out_shape=jax.ShapeDtypeStruct((copies, *value.shape), jnp.float32),
        in_specs=[pl.BlockSpec(memory_space=pl.ANY)],
        out_specs=pl.BlockSpec(memory_space=pltpu.HBM),
        scratch_shapes=[
            pltpu.VMEM(value.shape, jnp.float32),
            pltpu.SemaphoreType.DMA,
            pltpu.SemaphoreType.DMA((copies,)),
        ],
        cost_estimate=pl.CostEstimate(
            flops=price, bytes_accessed=4 * value.size * (1 + copies), transcendentals=0
        ),
        compiler_params=pltpu.CompilerParams(vmem_limit_bytes=ALL),
        name=name,
    )(value)


def add_kernel(order, residual, parts, out):
    x = lax.axis_index("col") // SIDE
    ys, _, columns = parts.shape
    each = columns // SIDE
    for place, step in enumerate(order):
        at = pl.ds(pl.multiple_of((x + step) % SIDE * columns, columns), columns)
        block = jnp.concatenate([parts[y, :, place * each : (place + 1) * each] for y in range(ys)], axis=1)
        out[:, at] = residual[:, at] + block


def add(order, residual, parts):
    import functools

    return pl.pallas_call(
        functools.partial(add_kernel, order),
        out_shape=jax.ShapeDtypeStruct(residual.shape, jnp.float32),
        in_specs=[pl.BlockSpec(memory_space=pltpu.VMEM)] * 2,
        out_specs=pl.BlockSpec(memory_space=pltpu.VMEM),
        compiler_params=pltpu.CompilerParams(vmem_limit_bytes=LIMIT),
        name="add_ladder",
    )(residual, parts)


def on_device(t, integrals, residual):
    v = integrals.reshape(integrals.shape[3:])
    rows = t.shape[0]

    def send(value, **move):
        return lax.ppermute(value, AXES, shifted(**move))

    half = rows // 2
    share = lax.dynamic_slice_in_dim(t, (1 - lax.axis_index("row") % 2) * half, half, 0)
    share_far = send(share, mirror=True)
    v_left, v_right = send(v, dx=1), send(v, dx=-1)
    near = lax.all_to_all(spread(t, SIDE, "spread_near"), "col", 0, 0, axis_index_groups=Y_RINGS)
    v_left, v_right, v_next = lax.optimization_barrier((v_left, v_right, v))
    v_across = send(v_next, dx=2)
    far = spread(share_far, 2 * SIDE, "spread_far", FAKE)
    far = lax.all_to_all(far, ("row", "col"), 0, 0, axis_index_groups=Y_RINGS_OF_TWO)
    near_pair = send(near, swap=True)
    order = (0, -1, 1, 2)
    blocks = (v, v_left, v_right, v_across)
    shape = (SIDE, rows, SIDE * v.shape[0])
    arrived = (gate((v_across,), GATE),)
    total = ladder(((0, 0), (0, 1)), None, (near, near_pair), blocks, shape, "ladder_near", PRICE, arrived, FETCH)
    far, total = lax.optimization_barrier((far, total))
    far_pair = send(far, swap=True)
    total = ladder(((1, 0),), total, (far,), blocks, shape, "ladder_far")
    total = ladder(((1, 1),), total, (far_pair,), blocks, shape, "ladder_far_pair")
    parts = lax.all_to_all(total, "col", 0, 0, axis_index_groups=Y_RINGS)
    return add(order, residual, parts)


def solution(mesh):
    return jax.shard_map(
        on_device,
        mesh=mesh,
        in_specs=(
            P("col", "layer"),
            P("row", "col", "layer", None, None),
            P("col", ("row", "layer")),
        ),
        out_specs=P("col", ("row", "layer")),
        check_vma=False,
    )
```
